256 devices in a mesh: seq: 32 (over x_lo, z, core), head: 8 (over y, x_hi).
Axes of the slice: x: 4 (x_hi: 2, x_lo: 2; x = x_hi * 2 + x_lo), y: 4, z: 8, core: 2. Of those that a mesh axis runs over, the one named last changes fastest.
Arguments:
- tokens: bfloat16 [16384, 4096], P('seq', 'head'), may hold values from -64 to 64
- norm_gain: float32 [4096], replicated, may hold values from 0.5 to 1.5
- w_query: bfloat16 [4096, 4096], P(None, 'head'), may hold values from -4 to 4
- w_key: bfloat16 [4096, 1024], P(None, 'head'), may hold values from -4 to 4
- w_value: bfloat16 [4096, 1024], P(None, 'head'), may hold values from -0.09375 to 0.09375
- w_output: bfloat16 [4096, 4096], P('head'), may hold values from -0.09375 to 0.09375
- widths: int32 [128], P('seq'), may hold values from 1 to 32
- dilation: int32 [128, 8], replicated, may hold values from 0 to 127, as said below
Outputs:
- layer_out: bfloat16 [16384, 4096], P('seq', 'head')
The draws below stay inside these ranges and needn't reach their ends.
Inputs may be any that keep to these rules, and one draw needn't show every extreme that they name: `dilation`: the 8 entries of one row differ. Over the 4 aligned rows of one index of seq, all entries that fall into the blocks of one index of seq (ids k * 4 to k * 4 + 3) name the same block. Row i names blocks of the indices 0 to max(i // 4, 8) - 1 of seq only.
All inputs are finite; a program needn't handle non-finite values.
Results may differ from the reference program's by a relative error of at most 0.005.
Values may be sent and summed in bfloat16 or wider, within the bound.
No kernel may reach another device: no remote copies, remote signals or barrier semaphores. Data moves between devices by JAX's collectives and lax.ppermute only.
A program may use at most 128 MiB of HBM per device.

```python
import math
import jax
import jax.numpy as jnp
from jax import lax

MODEL_WIDTH = 4096
QUERY_HEADS = 32
KEY_VALUE_HEADS = 8
HEAD_WIDTH = 128
BLOCK_TOKENS = 128
WINDOW_BLOCKS = 32
DILATION_COUNT = 8
QB_DEV = 4
NBLK = 128
TOKENS = 16384
QCOLS = 4096
KVCOLS = 1024


def draw_tokens(key, part):
    values = jax.random.normal(jax.random.fold_in(key, 4), (TOKENS, MODEL_WIDTH), jnp.float32)
    return jnp.clip(values, -64.0, 64.0).astype(jnp.bfloat16)


def key_projection_matrix(key):
    return jax.random.normal(jax.random.fold_in(key, 21), (MODEL_WIDTH, KEY_VALUE_HEADS * HEAD_WIDTH), jnp.float32) / math.sqrt(MODEL_WIDTH)


def draw_w_key(key, part):
    return jnp.clip(key_projection_matrix(key), -4.0, 4.0).astype(jnp.bfloat16)


def draw_w_query(key, part):
    noise_part = jax.random.normal(jax.random.fold_in(key, 22), (MODEL_WIDTH, QUERY_HEADS * HEAD_WIDTH), jnp.float32) / math.sqrt(MODEL_WIDTH)
    values = noise_part
    return jnp.clip(values, -4.0, 4.0).astype(jnp.bfloat16)


def draw_dilation(key, part):
    devices = NBLK // QB_DEV
    local_picks = jax.random.randint(jax.random.fold_in(key, 11), (devices, devices), 0, QB_DEV)
    scores = jax.random.randint(jax.random.fold_in(key, 12), (NBLK, devices), 0, 1 << 20)
    block_ids = jnp.arange(NBLK, dtype=jnp.int32)
    requester = block_ids // QB_DEV
    owner_limit = jnp.maximum(requester, DILATION_COUNT)
    owners = jnp.arange(devices, dtype=jnp.int32)
    ranked = scores * devices + owners[None, :] + jnp.where(owners[None, :] >= owner_limit[:, None], (1 << 20) * devices, 0)
    ordered = jnp.argsort(ranked, axis=1)[:, :DILATION_COUNT].astype(jnp.int32)
    chosen = local_picks[requester[:, None], ordered]
    return (ordered * QB_DEV + chosen).astype(jnp.int32)


def with_ends(drawn, own_key, low, high):
    dims = drawn.shape
    index_at = [jax.random.randint(jax.random.fold_in(own_key, axis), (), 0, dims[axis]) for axis in range(len(dims))]
    drawn = drawn.at[tuple(index_at)].set(low)
    longest = dims.index(max(dims))
    index_at[longest] = (index_at[longest] + 1) % dims[longest]
    return drawn.at[tuple(index_at)].set(high)


def block_scale(own_key, shape, pieces, low, top_value):
    def one(axis_at, blocks):
        steps = jax.random.uniform(jax.random.fold_in(jax.random.fold_in(own_key, 6), axis_at), (blocks,), jnp.float32, low / len(pieces), top_value / len(pieces))
        return jnp.repeat(jnp.exp(steps), shape[axis_at] // blocks).reshape((-1,) + (1,) * (len(shape) - axis_at - 1))

    level = one(*pieces[0])
    for cut in pieces[1:]:
        level = level * one(*cut)
    return level


def gaussian(key, shape, width, limit, shards=(), kind=jnp.bfloat16):
    drawn = jax.random.normal(key, shape, jnp.float32) * width
    if len(shards) > 0:
        drawn = block_scale(key, shape, shards, -0.22, 0.18) * drawn
    return jnp.clip(drawn, min=-limit, max=limit).astype(kind)


def setup_inputs(seed: int = 0) -> dict:
    arg_keys = jax.random.split(jax.random.key(seed), 9)
    tokens = draw_tokens(jax.random.fold_in(arg_keys[8], 71), 0)
    norm_gain = jnp.clip(1.0 + 0.1 * jax.random.normal(arg_keys[1], (MODEL_WIDTH,), jnp.float32), 0.5, 1.5)
    w_query = draw_w_query(jax.random.fold_in(arg_keys[8], 71), 0)
    w_key = draw_w_key(jax.random.fold_in(arg_keys[8], 71), 0)
    w_value = gaussian(arg_keys[4], (MODEL_WIDTH, KVCOLS), MODEL_WIDTH ** -0.5, 0.09375, ((1, 8),))
    w_output = gaussian(arg_keys[5], (QCOLS, MODEL_WIDTH), QCOLS ** -0.5, 0.09375, ((0, 8),))
    widths = with_ends(jax.random.randint(arg_keys[6], (NBLK,), 1, WINDOW_BLOCKS + 1), jax.random.fold_in(arg_keys[6], 1), 1, WINDOW_BLOCKS).astype(jnp.int32)
    dilation = draw_dilation(jax.random.fold_in(arg_keys[8], 71), 0)
    return {"tokens": tokens, "norm_gain": norm_gain, "w_query": w_query, "w_key": w_key, "w_value": w_value, "w_output": w_output, "widths": widths, "dilation": dilation}


EPSILON = 1e-05
NEGATIVE = -1e+30
ROPE_BASE = 10000.0

def rotary(values, positions, head_size):
    row_count = values.shape[0]
    head_count = values.shape[1] // head_size
    half_size = head_size // 2
    frequency = ROPE_BASE ** (-jnp.arange(half_size, dtype=jnp.float32) * 2.0 / head_size)
    angles = positions.astype(jnp.float32)[:, None] * frequency[None, :]
    cosine = jnp.cos(angles)[:, None, :]
    sine_part = jnp.sin(angles)[:, None, :]
    shaped = values.reshape(row_count, head_count, head_size)
    first_half = shaped[:, :, :half_size]
    second = shaped[:, :, half_size:]
    rotated = jnp.concatenate([first_half * cosine - second * sine_part, second * cosine + first_half * sine_part], axis=2)
    return rotated.reshape(row_count, head_count * head_size)

def rms_rows(tokens, norm_gain):
    values = tokens.astype(jnp.float32)
    scale_row = lax.rsqrt(lax.optimization_barrier(jnp.mean(values * values, axis=1, keepdims=True)) + EPSILON)
    return (values * scale_row * norm_gain[None, :]).astype(jnp.bfloat16)

def reference(tokens, norm_gain, w_query, w_key, w_value, w_output, widths, dilation):
    total_rows = tokens.shape[0]
    count_of_blocks = total_rows // BLOCK_TOKENS
    query_group_width = QUERY_HEADS // KEY_VALUE_HEADS
    normed = rms_rows(tokens, norm_gain)
    positions = jnp.arange(total_rows, dtype=jnp.int32)
    query_rows = rotary(jnp.dot(normed, w_query, preferred_element_type=jnp.float32), positions, HEAD_WIDTH).astype(jnp.bfloat16)
    key_row_list = rotary(jnp.dot(normed, w_key, preferred_element_type=jnp.float32), positions, HEAD_WIDTH).astype(jnp.bfloat16)
    value_row_list = jnp.dot(normed, w_value, preferred_element_type=jnp.float32).astype(jnp.bfloat16)
    leading_zero_rows = jnp.zeros(((WINDOW_BLOCKS - 1) * BLOCK_TOKENS, KEY_VALUE_HEADS * HEAD_WIDTH), jnp.bfloat16)
    key_padded = jnp.concatenate([leading_zero_rows, key_row_list], axis=0)
    value_padded = jnp.concatenate([leading_zero_rows, value_row_list], axis=0)
    blocked_keys = key_row_list.reshape(count_of_blocks, BLOCK_TOKENS, KEY_VALUE_HEADS * HEAD_WIDTH)
    blocked_values = value_row_list.reshape(count_of_blocks, BLOCK_TOKENS, KEY_VALUE_HEADS * HEAD_WIDTH)
    offsets = jnp.arange(BLOCK_TOKENS, dtype=jnp.int32)
    near_ids = jnp.arange(WINDOW_BLOCKS, dtype=jnp.int32) - (WINDOW_BLOCKS - 1)
    score_scale = 1.0 / math.sqrt(HEAD_WIDTH)

    def one_block(block_index):
        window_low = block_index - widths[block_index] + 1
        current_query_block = lax.dynamic_slice_in_dim(query_rows, block_index * BLOCK_TOKENS, BLOCK_TOKENS, 0)
        near_keys = lax.dynamic_slice_in_dim(key_padded, block_index * BLOCK_TOKENS, WINDOW_BLOCKS * BLOCK_TOKENS, 0)
        near_values = lax.dynamic_slice_in_dim(value_padded, block_index * BLOCK_TOKENS, WINDOW_BLOCKS * BLOCK_TOKENS, 0)
        distant_block_ids = dilation[block_index]
        distant_keys = jnp.take(blocked_keys, distant_block_ids, axis=0).reshape(DILATION_COUNT * BLOCK_TOKENS, KEY_VALUE_HEADS * HEAD_WIDTH)
        distant_values = jnp.take(blocked_values, distant_block_ids, axis=0).reshape(DILATION_COUNT * BLOCK_TOKENS, KEY_VALUE_HEADS * HEAD_WIDTH)
        key_slice = jnp.concatenate([near_keys, distant_keys], axis=0)
        value_slice = jnp.concatenate([near_values, distant_values], axis=0)
        block_ids = jnp.concatenate([block_index + near_ids, distant_block_ids])
        block_ok = jnp.concatenate([block_index + near_ids >= jnp.maximum(window_low, 0), distant_block_ids < window_low])
        key_pos = jnp.repeat(block_ids, BLOCK_TOKENS) * BLOCK_TOKENS + jnp.tile(offsets, WINDOW_BLOCKS + DILATION_COUNT)
        query_pos = block_index * BLOCK_TOKENS + offsets
        allowed = jnp.repeat(block_ok, BLOCK_TOKENS)[None, :] & (key_pos[None, :] <= query_pos[:, None])
        query_single_float = current_query_block.astype(jnp.float32).reshape(BLOCK_TOKENS, KEY_VALUE_HEADS, query_group_width, HEAD_WIDTH)
        key_single_float = key_slice.astype(jnp.float32).reshape(-1, KEY_VALUE_HEADS, HEAD_WIDTH)
        value_single_float = value_slice.astype(jnp.float32).reshape(-1, KEY_VALUE_HEADS, HEAD_WIDTH)
        scores = jnp.einsum('qhgd,khd->hgqk', query_single_float, key_single_float) * score_scale
        scores = jnp.where(allowed[None, None, :, :], scores, NEGATIVE)
        top_now = lax.optimization_barrier(jnp.max(scores, axis=3, keepdims=True))
        weights = jnp.exp(scores - top_now)
        total_sum = lax.optimization_barrier(jnp.sum(weights, axis=3))
        prob_bf = lax.optimization_barrier(weights.astype(jnp.bfloat16)).astype(jnp.float32)
        mixed = jnp.einsum('hgqk,khd->qhgd', prob_bf, value_single_float)
        mixed = mixed / jnp.transpose(total_sum, (2, 0, 1))[:, :, :, None]
        return mixed.reshape(BLOCK_TOKENS, QUERY_HEADS * HEAD_WIDTH)
    attention = lax.map(one_block, jnp.arange(count_of_blocks, dtype=jnp.int32))
    attention = attention.reshape(total_rows, QUERY_HEADS * HEAD_WIDTH).astype(jnp.bfloat16)
    projected = jnp.dot(attention, w_output, preferred_element_type=jnp.float32)
    return (tokens.astype(jnp.float32) + projected).astype(jnp.bfloat16)
```

```python
import functools
import math

import jax
import jax.numpy as jnp
from jax import lax
from jax.experimental import pallas as pl
from jax.experimental.pallas import tpu as pltpu
from jax.sharding import Mesh
from jax.sharding import PartitionSpec as P

MODEL_WIDTH = 4096
HEAD_WIDTH = 128
BLOCK = 128
DILATION_COUNT = 8
ROWS = 512
HALF = 256
QB = 4
SEQ = ("seq_0", "seq_1", "seq_2")
HEAD = ("head_0", "head_1")
YS, XS, ZS = 4, 2, 8
EPSILON = 1e-05
NEGATIVE = -1e30
ROPE_BASE = 10000.0
SCORE_FACTOR = math.log2(math.e) / math.sqrt(HEAD_WIDTH)
GROUP = 4


def moved(x, axis, size, step):
    return lax.ppermute(x, axis, [(k, (k + step) % size) for k in range(size)])


def y_up(x):
    return moved(x, "head_0", YS, 1)


def y_down(x):
    return moved(x, "head_0", YS, -1)


def x_flip(x):
    return moved(x, "head_1", XS, 1)


def z_up(x):
    return moved(x, "seq_1", ZS, 1)


def z_down(x):
    return moved(x, "seq_1", ZS, -1)


def pair_flip(x):
    return moved(x, "seq_0", 2, 1)


def core_flip(x):
    return moved(x, "seq_2", 2, 1)


def gather_features(a):
    n = a.shape[0] // 2
    b = x_flip(a)
    u = y_up(a)
    d = y_down(a)
    ct = y_up(u[:n])
    cb = y_down(d[n:])
    bu = y_up(b)
    bd = y_down(b)
    et = x_flip(ct)
    eb = x_flip(cb)
    return (a, b, u, d, bu, bd), (ct, cb, et, eb)


FEATURE_FROM = ((0, 0), (0, 1), (-1, 0), (1, 0), (-1, 1), (1, 1), (2, 0), (2, 1))


def gather_blocks(k):
    n = k.shape[0] // 2
    b = pair_flip(k)
    u1, d1 = z_up(k), z_down(k)
    u2, d2 = z_up(u1), z_down(d1)
    bu1, bd1 = z_up(b), z_down(b)
    u3, d3 = z_up(u2), z_down(d2)
    u4, d4 = z_up(u3[:n]), z_down(d3[n:])
    bu2, bd2 = z_up(bu1), z_down(bd1)
    bu3, bd3 = pair_flip(u3), pair_flip(d3)
    b4u, b4d = pair_flip(u4), pair_flip(d4)
    cat = lambda *v: jnp.concatenate(v, axis=0)
    own = (
        cat(k, b, u1, d1),
        cat(u2, d2, bu1, bd1),
        cat(u3, d3, bu2, bd2),
        cat(bu3, bd3, u4, d4, b4u, b4d),
    )
    return own, tuple(core_flip(g) for g in own)


BLOCK_FROM = (
    ((0, 0), (1, 0), (0, -1), (0, 1)),
    ((0, -2), (0, 2), (1, -1), (1, 1)),
    ((0, -3), (0, 3), (1, -2), (1, 2)),
    ((1, -3), (1, 3), (0, 4), (1, 4)),
)


def add_up(first, *rest):
    total = first.astype(jnp.float32)
    for r in rest:
        total = total + r.astype(jnp.float32)
    return total


def scatter_sums(part, residual):
    p = dict(zip(FEATURE_FROM, part))
    n = residual.shape[0] // 2
    bf = jnp.bfloat16
    far = x_flip(p[(2, 1)])
    from_low = y_up(p[(1, 1)])
    from_high = y_down(p[(-1, 1)])
    c = add_up(p[(2, 0)], far).astype(bf)
    c_low = y_up(c[:n])
    c_high = y_down(c[n:])
    rx = x_flip(add_up(p[(0, 1)], from_low, from_high).astype(bf))
    up = p[(1, 0)]
    down = p[(-1, 0)]
    up = jnp.concatenate([add_up(up[:n], c_low).astype(bf), up[n:]], axis=0)
    down = jnp.concatenate([down[:n], add_up(down[n:], c_high).astype(bf)], axis=0)
    ru = y_up(up)
    rd = y_down(down)
    return add_up(residual, p[(0, 0)], rx, ru, rd).astype(bf)


def dot_f32(a, b):
    return jnp.dot(a, b, preferred_element_type=jnp.float32)


def project(meta_ref, gain_ref, x_refs, half, weights):
    full, quarter = x_refs[:6], x_refs[6:]
    rows = pl.ds(half * HALF, HALF)
    pieces = [r[rows, :] for r in full] + [quarter[half][...], quarter[2 + half][...]]
    squares = jnp.zeros((HALF, 128), jnp.float32)
    sums = [jnp.zeros((HALF, w.shape[1]), jnp.float32) for w in weights]
    for k, piece in enumerate(pieces):
        h = meta_ref[k]
        x = piece.astype(jnp.float32)
        x2 = x * x
        for c in range(4):
            squares = squares + x2[:, c * 128 : (c + 1) * 128]
        scaled = (x * gain_ref[pl.ds(h, 1), :]).astype(jnp.bfloat16)
        span = pl.ds(pl.multiple_of(h * 512, 512), 512)
        for j, w in enumerate(weights):
            sums[j] = sums[j] + dot_f32(scaled, w[span, :])
    total = jnp.sum(squares, axis=1, keepdims=True)
    return sums, lax.rsqrt(total * (1.0 / MODEL_WIDTH) + EPSILON)


def rope(u, cos, sin):
    return u * cos + pltpu.roll(u, 64, 1) * sin


def kv_kernel(meta_ref, gain_ref, cos_ref, sin_ref, *refs):
    x_refs, (wk_ref, wv_ref, out_ref) = refs[:10], refs[10:]
    for half in range(2):
        rows = pl.ds(half * HALF, HALF)
        (k, v), scale = project(meta_ref, gain_ref, x_refs, half, (wk_ref, wv_ref))
        out_ref[rows, :128] = rope(k * scale, cos_ref[rows, :], sin_ref[rows, :]).astype(jnp.bfloat16)
        out_ref[rows, 128:] = (v * scale).astype(jnp.bfloat16)


def q_kernel(meta_ref, gain_ref, cos_ref, sin_ref, *refs):
    x_refs, (wq_ref, out_ref) = refs[:10], refs[10:]
    for half in range(2):
        rows = pl.ds(half * HALF, HALF)
        (q,), scale = project(meta_ref, gain_ref, x_refs, half, (wq_ref,))
        scale = scale * SCORE_FACTOR
        for g in range(4):
            cols = slice(g * 128, (g + 1) * 128)
            out_ref[rows, cols] = rope(
                q[:, cols] * scale, cos_ref[rows, :], sin_ref[rows, :]
            ).astype(jnp.bfloat16)


def out_kernel(meta_ref, at_ref, w_ref, *out_refs):
    for k, o in enumerate(out_refs):
        cols = pl.ds(pl.multiple_of(meta_ref[k] * 512, 512), 512)
        o[...] = dot_f32(at_ref[...], w_ref[:, cols]).astype(jnp.bfloat16)


def attention_kernel(
    meta_ref, dil_ref, width_ref, q_ref, *refs
):
    kv_in, out_ref, buf, acc, top, far, sems = refs[:8], refs[8], refs[9], refs[10], refs[11], refs[12], refs[13]
    first_block = meta_ref[0]
    copies = []
    for g in range(8):
        for s in range(4):
            slot = g * 4 + s
            dest = pl.multiple_of(meta_ref[1 + slot] * ROWS, ROWS)
            c = pltpu.make_async_copy(
                kv_in[g].at[pl.ds(s * ROWS, ROWS), :], buf.at[pl.ds(dest, ROWS), :], sems.at[slot]
            )
            c.start()
            copies.append(c)
    for c in copies:
        c.wait()
    ones = jnp.ones((GROUP * BLOCK, 128), jnp.bfloat16)

    def load(blocks):
        keys, values = [], []
        for b in blocks:
            r = pl.ds(pl.multiple_of(b * BLOCK, BLOCK), BLOCK)
            keys.append(buf[r, :128])
            values.append(buf[r, 128:])
        values = jnp.concatenate(values, axis=0)
        return jnp.concatenate(keys, axis=0), jnp.concatenate([values, ones], axis=1)

    def one_block(j, _):
        i = first_block + j
        low = i - width_ref[j] + 1
        start = jnp.maximum(low, 0)
        count = jnp.int32(0)
        for e in range(DILATION_COUNT):
            b = dil_ref[i, e]
            far[count] = b
            count = count + jnp.where(b < low, 1, 0)
        total = count + i - start
        rest = lax.rem(total, GROUP)
        rows = pl.ds(pl.multiple_of(j * BLOCK, BLOCK), BLOCK)

        def block_at(t):
            return jnp.where(t < count, far[jnp.minimum(t, DILATION_COUNT - 1)], start + t - count)

        def queries(half):
            return jnp.concatenate(
                [q_ref[rows, c * 128 : (c + 1) * 128] for c in (2 * half, 2 * half + 1)], axis=0
            )

        keys, values = load(
            [i] + [jnp.where(t < rest, block_at(jnp.int32(t)), i) for t in range(GROUP - 1)]
        )
        shape = (2 * BLOCK, GROUP * BLOCK)
        col = lax.broadcasted_iota(jnp.int32, shape, 1)
        row = lax.broadcasted_iota(jnp.int32, shape, 0) & (BLOCK - 1)
        limit = jnp.where(col < BLOCK, row + 1, (1 + rest) * BLOCK)
        for half in range(2):
            s = lax.dot_general(
                queries(half), keys, (((1,), (1,)), ((), ())), preferred_element_type=jnp.float32
            )
            s = jnp.where(col < limit, s, NEGATIVE)
            m = jnp.max(s, axis=1, keepdims=True)
            p = jnp.exp2(s - m).astype(jnp.bfloat16)
            acc[half] = dot_f32(p, values)
            top[half] = jnp.broadcast_to(m, (2 * BLOCK, 128))

        def step(g, _):
            t = rest + g * GROUP
            keys, values = load([block_at(t + e) for e in range(GROUP)])
            for half in range(2):
                s = lax.dot_general(
                    queries(half), keys, (((1,), (1,)), ((), ())), preferred_element_type=jnp.float32
                )
                old = top[half]
                new = jnp.maximum(old, jnp.max(s, axis=1, keepdims=True))
                fade = jnp.exp2(old - new)
                p = jnp.exp2(s - jnp.concatenate([new] * GROUP, axis=1)).astype(jnp.bfloat16)
                acc[half] = acc[half] * jnp.concatenate([fade] * 2, axis=1) + dot_f32(p, values)
                top[half] = new
            return 0

        lax.fori_loop(0, lax.div(total, GROUP), step, 0)
        for half in range(2):
            a = acc[half]
            o = (a[:, :128] / a[:, 128:]).astype(jnp.bfloat16)
            out_ref[rows, (2 * half) * 128 : (2 * half + 1) * 128] = o[:BLOCK]
            out_ref[rows, (2 * half + 1) * 128 : (2 * half + 2) * 128] = o[BLOCK:]
        return 0

    lax.fori_loop(0, QB, one_block, 0)


VMEM = pl.BlockSpec(memory_space=pltpu.VMEM)
SMEM = pl.BlockSpec(memory_space=pltpu.SMEM)
ANY = pl.BlockSpec(memory_space=pl.ANY)
bf16 = jnp.bfloat16


def local_attention(meta, dilation, widths, q, groups, interpret=False):
    return pl.pallas_call(
        attention_kernel,
        out_shape=jax.ShapeDtypeStruct((ROWS, 512), bf16),
        in_specs=[SMEM] * 3 + [VMEM] + [ANY] * 8,
        out_specs=VMEM,
        scratch_shapes=[
            pltpu.VMEM((32 * ROWS, 256), bf16),
            pltpu.VMEM((2, 2 * BLOCK, 256), jnp.float32),
            pltpu.VMEM((2, 2 * BLOCK, 128), jnp.float32),
            pltpu.SMEM((DILATION_COUNT + 1,), jnp.int32),
            pltpu.SemaphoreType.DMA((32,)),
        ],
        interpret=interpret,
        name="attend",
    )(meta, dilation, widths, q, *groups)


def shards(tokens, norm_gain, w_query, w_key, w_value, w_output, widths, dilation):
    x0, z, core = (lax.axis_index(a) for a in SEQ)
    y, xh = (lax.axis_index(a) for a in HEAD)
    seq_index = (x0 * ZS + z) * 2 + core
    first_block = seq_index * QB
    dy = jnp.array([d for d, _ in FEATURE_FROM], jnp.int32)
    dx = jnp.array([d for _, d in FEATURE_FROM], jnp.int32)
    heads = ((y + dy + YS) % YS) * XS + (xh + dx) % XS
    bx = jnp.array([d for g in BLOCK_FROM for d, _ in g], jnp.int32)
    bz = jnp.array([d for g in BLOCK_FROM for _, d in g], jnp.int32)
    owners = ((x0 + bx) % 2 * ZS + (z + bz + ZS) % ZS) * 2
    owners = jnp.concatenate(
        [first_block[None], owners + core, owners + (1 - core)]
    ).astype(jnp.int32)

    half_size = HEAD_WIDTH // 2
    positions = first_block * BLOCK + jnp.arange(ROWS, dtype=jnp.int32)
    frequency = ROPE_BASE ** (-jnp.arange(half_size, dtype=jnp.float32) * 2.0 / HEAD_WIDTH)
    angles = positions.astype(jnp.float32)[:, None] * frequency[None, :]
    cosine, sine = jnp.cos(angles), jnp.sin(angles)
    cosine = jnp.concatenate([cosine, cosine], axis=1)
    sine = jnp.concatenate([-sine, sine], axis=1)
    gain = norm_gain.reshape(8, 512)

    full, quarter = gather_features(tokens)
    pieces = full + quarter
    kv = pl.pallas_call(
        kv_kernel,
        out_shape=jax.ShapeDtypeStruct((ROWS, 256), bf16),
        in_specs=[SMEM] + [VMEM] * 15,
        out_specs=VMEM,
        name="keys_values",
    )(heads, gain, cosine, sine, *pieces, w_key, w_value)
    own, swapped = gather_blocks(kv)
    q = pl.pallas_call(
        q_kernel,
        out_shape=jax.ShapeDtypeStruct((ROWS, 512), bf16),
        in_specs=[SMEM] + [VMEM] * 14,
        out_specs=VMEM,
        name="queries",
    )(heads, gain, cosine, sine, *pieces, w_query)
    attention = local_attention(owners, dilation, widths, q, own + swapped)

    def shares(which):
        return pl.pallas_call(
            out_kernel,
            out_shape=[jax.ShapeDtypeStruct((ROWS, 512), bf16)] * len(which),
            in_specs=[SMEM, VMEM, VMEM],
            out_specs=[VMEM] * len(which),
            name="project_out",
        )(jnp.stack([heads[k] for k in which]), attention, w_output)

    first = (7, 4, 5)
    second = (6, 1, 2, 3, 0)
    part = dict(zip(first, shares(first)))
    part.update(zip(second, shares(second)))
    return scatter_sums([part[k] for k in range(8)], tokens)


def solution(mesh):
    split = Mesh(mesh.devices.reshape(2, ZS, 2, YS, XS), SEQ + HEAD)
    placed = (
        P(SEQ, HEAD),
        P(),
        P(None, HEAD),
        P(None, HEAD),
        P(None, HEAD),
        P(HEAD, None),
        P(SEQ),
        P(),
    )
    return jax.shard_map(
        shards, mesh=split, in_specs=placed, out_specs=P(SEQ, HEAD), check_vma=False
    )
```

```python
import functools
import math

import jax
import jax.numpy as jnp
from jax import lax
from jax.experimental import pallas as pl
from jax.experimental.pallas import tpu as pltpu
from jax.sharding import Mesh
from jax.sharding import PartitionSpec as P

MODEL_WIDTH = 4096
HEAD_WIDTH = 128
BLOCK = 128
DILATION_COUNT = 8
ROWS = 512
HALF = 256
QB = 4
SEQ = ("seq_0", "seq_1", "seq_2")
HEAD = ("head_0", "head_1")
YS, XS, ZS = 4, 2, 8
EPSILON = 1e-05
NEGATIVE = -1e30
ROPE_BASE = 10000.0
SCORE_FACTOR = math.log2(math.e) / math.sqrt(HEAD_WIDTH)
GROUP = 4


def moved(x, axis, size, step):
    return lax.ppermute(x, axis, [(k, (k + step) % size) for k in range(size)])


def y_up(x):
    return moved(x, "head_0", YS, 1)


def y_down(x):
    return moved(x, "head_0", YS, -1)


def x_flip(x):
    return moved(x, "head_1", XS, 1)


def pair_flip(x):
    return moved(x, "seq_0", 2, 1)


def core_flip(x):
    return moved(x, "seq_2", 2, 1)


def gather_features(a):
    n = a.shape[0] // 2
    b = x_flip(a)
    u = y_up(a)
    d = y_down(a)
    ct = y_up(u[:n])
    cb = y_down(d[n:])
    bu = y_up(b)
    bd = y_down(b)
    et = x_flip(ct)
    eb = x_flip(cb)
    return (a, b, u, d, bu, bd), (ct, cb, et, eb)


FEATURE_FROM = ((0, 0), (0, 1), (-1, 0), (1, 0), (-1, 1), (1, 1), (2, 0), (2, 1))


def ring(x):
    pairs = []
    for z in range(ZS):
        pairs.append((2 * z, 2 * ((z + 1) % ZS)))
        pairs.append((2 * z + 1, 2 * ((z - 1) % ZS) + 1))
    return lax.ppermute(x, ("seq_1", "seq_2"), pairs)


def cat(*v):
    return jnp.concatenate(v, axis=0)


def gather_blocks(k):
    n = k.shape[0]
    k2 = cat(k, core_flip(k))
    b = pair_flip(k)
    r1 = ring(k2)
    b2 = cat(b, core_flip(b))
    r2 = ring(r1)
    rb1 = ring(b2)
    r3 = ring(r2)
    s1 = core_flip(cat(r1, r2))
    rb2 = ring(rb1)
    r4 = ring(r3[:n])
    f3 = pair_flip(r3)
    s2 = core_flip(cat(rb1, r3, r4))
    f4 = pair_flip(r4)
    s3 = core_flip(cat(rb2, f3, f4))
    return k2, b2, r1, r2, rb1, r3, r4, rb2, f3, f4, s1, s2, s3


PARTS_OF = {
    "k2": ((0, 0, 0), (0, 0, 1)),
    "b2": ((1, 0, 0), (1, 0, 1)),
    "r1": ((0, 1, 0), (0, 1, 1)),
    "r2": ((0, 2, 0), (0, 2, 1)),
    "rb1": ((1, 1, 0), (1, 1, 1)),
    "r3": ((0, 3, 0), (0, 3, 1)),
    "r4": ((0, 4, 0),),
    "rb2": ((1, 2, 0), (1, 2, 1)),
    "f3": ((1, 3, 0), (1, 3, 1)),
    "f4": ((1, 4, 0),),
}
BLOCK_FROM = tuple(
    tuple((dx, steps, c, 0) for dx, steps, c in PARTS_OF[name])
    for name in ("k2", "b2", "r1", "r2", "rb1", "r3", "r4", "rb2", "f3", "f4")
) + tuple(
    tuple((dx, steps, 1 - c, 1) for name in names for dx, steps, c in PARTS_OF[name])
    for names in (("r1", "r2"), ("rb1", "r3", "r4"), ("rb2", "f3", "f4"))
)


def seq_at(x0, z, core, part):
    dx, steps, other, far_ring = part
    turn = jnp.where((core + far_ring) % 2 == 0, ZS - steps, steps)
    return ((x0 + dx) % 2 * ZS + (z + turn) % ZS) * 2 + (core + other) % 2


def add_up(first, *rest):
    total = first.astype(jnp.float32)
    for r in rest:
        total = total + r.astype(jnp.float32)
    return total


def scatter_sums(part, residual):
    p = dict(zip(FEATURE_FROM, part))
    n = residual.shape[0] // 2
    bf = jnp.bfloat16
    far = x_flip(p[(2, 1)])
    from_low = y_up(p[(1, 1)])
    from_high = y_down(p[(-1, 1)])
    c = add_up(p[(2, 0)], far).astype(bf)
    c_low = y_up(c[:n])
    c_high = y_down(c[n:])
    rx = x_flip(add_up(p[(0, 1)], from_low, from_high).astype(bf))
    up = p[(1, 0)]
    down = p[(-1, 0)]
    up = jnp.concatenate([add_up(up[:n], c_low).astype(bf), up[n:]], axis=0)
    down = jnp.concatenate([down[:n], add_up(down[n:], c_high).astype(bf)], axis=0)
    ru = y_up(up)
    rd = y_down(down)
    return add_up(residual, p[(0, 0)], rx, ru, rd).astype(bf)


def dot_f32(a, b):
    return jnp.dot(a, b, preferred_element_type=jnp.float32)


def seq_place():
    return tuple(lax.axis_index(a) for a in SEQ)


def first_block_here():
    x0, z, core = seq_place()
    return ((x0 * ZS + z) * 2 + core) * QB


def head_at(part):
    y, xh = lax.axis_index("head_0"), lax.axis_index("head_1")
    dy, dx = part
    return (y + (dy + YS) % YS) % YS * XS + (xh + dx) % XS


def joined(quarter, whole):
    for k in range(2):
        for half in range(2):
            whole[k, half * HALF : (half + 1) * HALF, :] = quarter[2 * k + half][...]


def project(gain_ref, full, whole, rows, weights):
    squares = jnp.zeros((HALF, 128), jnp.float32)
    sums = [jnp.zeros((HALF, w.shape[1]), jnp.float32) for w in weights]
    for k, part in enumerate(FEATURE_FROM):
        piece = full[k][rows, :] if k < 6 else whole[k - 6, rows, :]
        h = head_at(part)
        x = piece.astype(jnp.float32)
        x2 = x * x
        for c in range(4):
            squares = squares + x2[:, c * 128 : (c + 1) * 128]
        scaled = (x * gain_ref[pl.ds(h, 1), :]).astype(jnp.bfloat16)
        span = pl.ds(pl.multiple_of(h * 512, 512), 512)
        for j, w in enumerate(weights):
            sums[j] = sums[j] + dot_f32(scaled, w[span, :])
    total = jnp.sum(squares, axis=1, keepdims=True)
    return sums, lax.rsqrt(total * (1.0 / MODEL_WIDTH) + EPSILON)


def rope(u, cos, sin):
    return u * cos + pltpu.roll(u, 64, 1) * sin


def kv_kernel(gain_ref, cos_ref, sin_ref, *refs):
    full, quarter, (wk_ref, wv_ref, out_ref, whole) = refs[:6], refs[6:10], refs[10:]
    joined(quarter, whole)

    def body(half, _):
        rows = pl.ds(pl.multiple_of(half * HALF, HALF), HALF)
        (k, v), scale = project(gain_ref, full, whole, rows, (wk_ref, wv_ref))
        out_ref[rows, :128] = rope(k * scale, cos_ref[rows, :], sin_ref[rows, :]).astype(jnp.bfloat16)
        out_ref[rows, 128:] = (v * scale).astype(jnp.bfloat16)
        return 0

    lax.fori_loop(0, 2, body, 0)


def q_kernel(gain_ref, dil_ref, width_ref, cos_ref, sin_ref, *refs):
    full, quarter, (wq_ref, out_ref, list_ref, whole) = refs[:6], refs[6:10], refs[10:]
    joined(quarter, whole)
    first = first_block_here()
    for j in range(QB):
        i = first + j
        low = i - width_ref[j] + 1
        start = jnp.maximum(low, 0)
        count = jnp.int32(0)
        for e in range(DILATION_COUNT):
            b = dil_ref[i, e]
            list_ref[j, 1 + count] = b
            count = count + jnp.where(b < low, 1, 0)

        def near(t, _):
            list_ref[j, 1 + count + t] = start + t
            return 0

        lax.fori_loop(0, i - start, near, 0)
        list_ref[j, 0] = count + i - start

    def body(half, _):
        rows = pl.ds(pl.multiple_of(half * HALF, HALF), HALF)
        (q,), scale = project(gain_ref, full, whole, rows, (wq_ref,))
        scale = scale * SCORE_FACTOR
        for g in range(4):
            cols = slice(g * 128, (g + 1) * 128)
            out_ref[rows, cols] = rope(
                q[:, cols] * scale, cos_ref[rows, :], sin_ref[rows, :]
            ).astype(jnp.bfloat16)
        return 0

    lax.fori_loop(0, 2, body, 0)


def out_kernel(which, at_ref, w_ref, *out_refs):
    for k, o in zip(which, out_refs):
        cols = pl.ds(pl.multiple_of(head_at(FEATURE_FROM[k]) * 512, 512), 512)
        o[...] = dot_f32(at_ref[...], w_ref[:, cols]).astype(jnp.bfloat16)


def attention_kernel(list_ref, q_ref, *refs):
    kv_in, (out_ref, buf, acc, top, sems) = refs[: len(BLOCK_FROM)], refs[len(BLOCK_FROM) :]
    x0, z, core = seq_place()
    first_block = first_block_here()
    copies = []
    for ref, parts in zip(kv_in, BLOCK_FROM):
        for s, part in enumerate(parts):
            dest = pl.multiple_of(seq_at(x0, z, core, part) * ROWS, ROWS)
            c = pltpu.make_async_copy(
                ref.at[pl.ds(s * ROWS, ROWS), :], buf.at[pl.ds(dest, ROWS), :], sems.at[len(copies)]
            )
            c.start()
            copies.append(c)
    for c in copies:
        c.wait()
    ones = jnp.ones((GROUP * BLOCK, 128), jnp.bfloat16)

    def load(blocks):
        keys, values = [], []
        for b in blocks:
            r = pl.ds(pl.multiple_of(b * BLOCK, BLOCK), BLOCK)
            keys.append(buf[r, :128])
            values.append(buf[r, 128:])
        values = jnp.concatenate(values, axis=0)
        return jnp.concatenate(keys, axis=0), jnp.concatenate([values, ones], axis=1)

    def one_block(j, _):
        i = first_block + j
        total = list_ref[j, 0]
        rest = lax.rem(total, GROUP)
        rows = pl.ds(pl.multiple_of(j * BLOCK, BLOCK), BLOCK)

        def queries(half):
            return jnp.concatenate(
                [q_ref[rows, c * 128 : (c + 1) * 128] for c in (2 * half, 2 * half + 1)], axis=0
            )

        keys, values = load(
            [i] + [jnp.where(t < rest, list_ref[j, 1 + t], i) for t in range(GROUP - 1)]
        )
        shape = (2 * BLOCK, GROUP * BLOCK)
        col = lax.broadcasted_iota(jnp.int32, shape, 1)
        row = lax.broadcasted_iota(jnp.int32, shape, 0) & (BLOCK - 1)
        limit = jnp.where(col < BLOCK, row + 1, (1 + rest) * BLOCK)
        for half in range(2):
            s = lax.dot_general(
                queries(half), keys, (((1,), (1,)), ((), ())), preferred_element_type=jnp.float32
            )
            s = jnp.where(col < limit, s, NEGATIVE)
            m = jnp.max(s, axis=1, keepdims=True)
            p = jnp.exp2(s - m).astype(jnp.bfloat16)
            acc[half] = dot_f32(p, values)
            top[half] = jnp.broadcast_to(m, (2 * BLOCK, 128))

        def step(g, _):
            t = 1 + rest + g * GROUP
            keys, values = load([list_ref[j, t + e] for e in range(GROUP)])
            for half in range(2):
                s = lax.dot_general(
                    queries(half), keys, (((1,), (1,)), ((), ())), preferred_element_type=jnp.float32
                )
                old = top[half]
                new = jnp.maximum(old, jnp.max(s, axis=1, keepdims=True))
                fade = jnp.exp2(old - new)
                p = jnp.exp2(s - jnp.concatenate([new] * GROUP, axis=1)).astype(jnp.bfloat16)
                acc[half] = acc[half] * jnp.concatenate([fade] * 2, axis=1) + dot_f32(p, values)
                top[half] = new
            return 0

        lax.fori_loop(0, lax.div(total, GROUP), step, 0)
        for half in range(2):
            a = acc[half]
            o = (a[:, :128] / a[:, 128:]).astype(jnp.bfloat16)
            out_ref[rows, (2 * half) * 128 : (2 * half + 1) * 128] = o[:BLOCK]
            out_ref[rows, (2 * half + 1) * 128 : (2 * half + 2) * 128] = o[BLOCK:]
        return 0

    lax.fori_loop(0, QB, one_block, 0)


VMEM = pl.BlockSpec(memory_space=pltpu.VMEM)
SMEM = pl.BlockSpec(memory_space=pltpu.SMEM)
ANY = pl.BlockSpec(memory_space=pl.ANY)
bf16 = jnp.bfloat16


def local_attention(lists, q, gathered):
    return pl.pallas_call(
        attention_kernel,
        out_shape=jax.ShapeDtypeStruct((ROWS, 512), bf16),
        in_specs=[SMEM, VMEM] + [ANY] * len(gathered),
        out_specs=VMEM,
        scratch_shapes=[
            pltpu.VMEM((32 * ROWS, 256), bf16),
            pltpu.VMEM((2, 2 * BLOCK, 256), jnp.float32),
            pltpu.VMEM((2, 2 * BLOCK, 128), jnp.float32),
            pltpu.SemaphoreType.DMA((32,)),
        ],
        cost_estimate=pl.CostEstimate(flops=2 * 10**10, transcendentals=10**7, bytes_accessed=10**7),
        name="attend",
    )(lists, q, *gathered)


def shards(tokens, norm_gain, w_query, w_key, w_value, w_output, widths, dilation):
    half_size = HEAD_WIDTH // 2
    positions = first_block_here() * BLOCK + jnp.arange(ROWS, dtype=jnp.int32)
    frequency = ROPE_BASE ** (-jnp.arange(half_size, dtype=jnp.float32) * 2.0 / HEAD_WIDTH)
    angles = positions.astype(jnp.float32)[:, None] * frequency[None, :]
    cosine, sine = jnp.cos(angles), jnp.sin(angles)
    cosine = jnp.concatenate([cosine, cosine], axis=1)
    sine = jnp.concatenate([-sine, sine], axis=1)
    gain = norm_gain.reshape(8, 512)

    full, quarter = gather_features(tokens)
    pieces = full + quarter
    kv = pl.pallas_call(
        kv_kernel,
        out_shape=jax.ShapeDtypeStruct((ROWS, 256), bf16),
        in_specs=[VMEM] * 15,
        out_specs=VMEM,
        scratch_shapes=[pltpu.VMEM((2, ROWS, 512), bf16)],
        cost_estimate=pl.CostEstimate(flops=10**9, transcendentals=0, bytes_accessed=6 * 10**6),
        name="keys_values",
    )(gain, cosine, sine, *pieces, w_key, w_value)
    gathered = gather_blocks(kv)
    query_call = pl.pallas_call(
        q_kernel,
        out_shape=[
            jax.ShapeDtypeStruct((ROWS, 512), bf16),
            jax.ShapeDtypeStruct((QB, 64), jnp.int32),
        ],
        in_specs=[VMEM] + [SMEM] * 2 + [VMEM] * 13,
        out_specs=[VMEM, SMEM],
        scratch_shapes=[pltpu.VMEM((2, ROWS, 512), bf16)],
        cost_estimate=pl.CostEstimate(flops=4 * 10**9, transcendentals=0, bytes_accessed=10**7),
        name="queries",
    )
    q, lists = query_call(gain, dilation, widths, cosine, sine, *pieces, w_query)
    attention = local_attention(lists, q, gathered)

    def shares(which):
        return pl.pallas_call(
            functools.partial(out_kernel, which),
            out_shape=[jax.ShapeDtypeStruct((ROWS, 512), bf16)] * len(which),
            in_specs=[VMEM, VMEM],
            out_specs=[VMEM] * len(which),
            cost_estimate=pl.CostEstimate(
                flops=len(which) * 2**28, transcendentals=0, bytes_accessed=len(which) * 2**20
            ),
            name="project_out",
        )(attention, w_output)

    first = (7, 4, 5)
    second = (6, 1, 2, 3, 0)
    part = dict(zip(first, shares(first)))
    part.update(zip(second, shares(second)))
    return scatter_sums([part[k] for k in range(8)], tokens)


def solution(mesh):
    split = Mesh(mesh.devices.reshape(2, ZS, 2, YS, XS), SEQ + HEAD)
    placed = (
        P(SEQ, HEAD),
        P(),
        P(None, HEAD),
        P(None, HEAD),
        P(None, HEAD),
        P(HEAD, None),
        P(SEQ),
        P(),
    )
    return jax.shard_map(
        shards, mesh=split, in_specs=placed, out_specs=P(SEQ, HEAD), check_vma=False
    )
```

```python
import functools
import math

import jax
import jax.numpy as jnp
from jax import lax
from jax.experimental import pallas as pl
from jax.experimental.pallas import tpu as pltpu
from jax.sharding import Mesh
from jax.sharding import PartitionSpec as P

MODEL_WIDTH = 4096
HEAD_WIDTH = 128
BLOCK = 128
DILATION_COUNT = 8
ROWS = 512
HALF = 256
QB = 4
SEQ = ("seq_0", "seq_1", "seq_2")
HEAD = ("head_0", "head_1")
YS, XS, ZS = 4, 2, 8
EPSILON = 1e-05
NEGATIVE = -1e30
ROPE_BASE = 10000.0
SCORE_FACTOR = math.log2(math.e) / math.sqrt(HEAD_WIDTH)
GROUP = 4
LATE = 64


def moved(x, axis, size, step):
    return lax.ppermute(x, axis, [(k, (k + step) % size) for k in range(size)])


def y_up(x):
    return moved(x, "head_0", YS, 1)


def y_down(x):
    return moved(x, "head_0", YS, -1)


def x_flip(x):
    return moved(x, "head_1", XS, 1)


def pair_flip(x):
    return moved(x, "seq_0", 2, 1)


def core_flip(x):
    return moved(x, "seq_2", 2, 1)


def gather_features(a):
    n = a.shape[0] // 2
    b = x_flip(a)
    u = y_up(a)
    d = y_down(a)
    ct = y_up(u[:n])
    cb = y_down(d[n:])
    bu = y_up(b)
    bd = y_down(b)
    et = x_flip(ct)
    eb = x_flip(cb)
    return (a, b, u, d, bu, bd), (ct, cb, et, eb)


FEATURE_FROM = ((0, 0), (0, 1), (-1, 0), (1, 0), (-1, 1), (1, 1), (2, 0), (2, 1))


def ring(x):
    pairs = []
    for z in range(ZS):
        pairs.append((2 * z, 2 * ((z + 1) % ZS)))
        pairs.append((2 * z + 1, 2 * ((z - 1) % ZS) + 1))
    return lax.ppermute(x, ("seq_1", "seq_2"), pairs)


def cat(*v):
    return jnp.concatenate(v, axis=0)


def gather_blocks(k):
    n = k.shape[0]
    k2 = cat(k, core_flip(k))
    b = pair_flip(k)
    r1 = ring(k2)
    b2 = cat(b, core_flip(b))
    r2 = ring(r1)
    rb1 = ring(b2)
    r3 = ring(r2)
    s1 = core_flip(cat(r1, r2))
    rb2 = ring(rb1)
    r4 = ring(r3[:n])
    f3 = pair_flip(r3)
    s2 = core_flip(cat(rb1, r3))
    f4 = pair_flip(r4)
    s3 = core_flip(cat(rb2, r4))
    s4 = core_flip(cat(f3, f4))
    return (k2, b2, r1, r2, rb1, s1), (r3, r4, rb2, f3, f4, s2, s3, s4)


PARTS_OF = {
    "k2": ((0, 0, 0), (0, 0, 1)),
    "b2": ((1, 0, 0), (1, 0, 1)),
    "r1": ((0, 1, 0), (0, 1, 1)),
    "r2": ((0, 2, 0), (0, 2, 1)),
    "rb1": ((1, 1, 0), (1, 1, 1)),
    "r3": ((0, 3, 0), (0, 3, 1)),
    "r4": ((0, 4, 0),),
    "rb2": ((1, 2, 0), (1, 2, 1)),
    "f3": ((1, 3, 0), (1, 3, 1)),
    "f4": ((1, 4, 0),),
}


def own_parts(*names):
    return tuple(tuple((dx, n, c, 0) for dx, n, c in PARTS_OF[name]) for name in names)


def other_parts(*names):
    return tuple((dx, n, 1 - c, 1) for name in names for dx, n, c in PARTS_OF[name])


EARLY_FROM = own_parts("k2", "b2", "r1", "r2", "rb1") + (other_parts("r1", "r2"),)
LATE_FROM = own_parts("r3", "r4", "rb2", "f3", "f4") + (
    other_parts("rb1", "r3"),
    other_parts("rb2", "r4"),
    other_parts("f3", "f4"),
)


def seq_at(x0, z, core, part):
    dx, steps, other, far_ring = part
    turn = jnp.where((core + far_ring) & 1 == 0, ZS - steps, steps)
    return (((x0 + dx) & 1) * ZS + ((z + turn) & (ZS - 1))) * 2 + ((core + other) & 1)


def add_up(first, *rest):
    total = first.astype(jnp.float32)
    for r in rest:
        total = total + r.astype(jnp.float32)
    return total


def scatter_sums(part, residual):
    p = dict(zip(FEATURE_FROM, part))
    n = residual.shape[0] // 2
    bf = jnp.bfloat16
    far = x_flip(p[(2, 1)])
    from_low = y_up(p[(1, 1)])
    from_high = y_down(p[(-1, 1)])
    c = add_up(p[(2, 0)], far).astype(bf)
    c_low = y_up(c[:n])
    c_high = y_down(c[n:])
    rx = x_flip(add_up(p[(0, 1)], from_low, from_high).astype(bf))
    up = p[(1, 0)]
    down = p[(-1, 0)]
    up = jnp.concatenate([add_up(up[:n], c_low).astype(bf), up[n:]], axis=0)
    down = jnp.concatenate([down[:n], add_up(down[n:], c_high).astype(bf)], axis=0)
    ru = y_up(up)
    rd = y_down(down)
    return add_up(residual, p[(0, 0)], rx, ru, rd).astype(bf)


def dot_f32(a, b):
    return jnp.dot(a, b, preferred_element_type=jnp.float32)


def seq_place():
    return tuple(lax.axis_index(a) for a in SEQ)


def first_block_here():
    x0, z, core = seq_place()
    return ((x0 * ZS + z) * 2 + core) * QB


def head_at(part):
    y, xh = lax.axis_index("head_0"), lax.axis_index("head_1")
    dy, dx = part
    return ((y + dy + YS) & (YS - 1)) * XS + ((xh + dx) & (XS - 1))


def fetch_features(refs, xbuf, sems):
    n = 0
    copies = []
    for k, part in enumerate(FEATURE_FROM):
        place = xbuf.at[head_at(part)]
        pieces = [(refs[k], place)] if k < 6 else [
            (refs[2 * k - 6 + half], place.at[pl.ds(half * HALF, HALF), :]) for half in range(2)
        ]
        for source, target in pieces:
            c = pltpu.make_async_copy(source, target, sems.at[n])
            c.start()
            copies.append(c)
            n += 1
    for c in copies:
        c.wait()


def project(xbuf, gain_ref, rows, weights, sums, squares):
    squares[...] = jnp.zeros_like(squares)
    for a in sums:
        a[...] = jnp.zeros_like(a)

    def block(h, _):
        x = xbuf[h, rows, :].astype(jnp.float32)
        x2 = x * x
        squares[...] += sum(x2[:, c * 128 : (c + 1) * 128] for c in range(4))
        scaled = (x * gain_ref[pl.ds(h, 1), :]).astype(jnp.bfloat16)
        span = pl.ds(pl.multiple_of(h * 512, 512), 512)
        for a, w in zip(sums, weights):
            a[...] += dot_f32(scaled, w[span, :])
        return 0

    lax.fori_loop(0, 8, block, 0)
    total = jnp.sum(squares[...], axis=1, keepdims=True)
    return lax.rsqrt(total * (1.0 / MODEL_WIDTH) + EPSILON)


def rope(u, cos, sin):
    return u * cos + pltpu.roll(u, 64, 1) * sin


def kv_kernel(gain_ref, cos_ref, sin_ref, *refs):
    x_refs, (wk_ref, wv_ref, out_ref, xbuf, k_sum, v_sum, squares, sems) = refs[:10], refs[10:]
    fetch_features(x_refs, xbuf, sems)

    def body(half, _):
        rows = pl.ds(pl.multiple_of(half * HALF, HALF), HALF)
        scale = project(xbuf, gain_ref, rows, (wk_ref, wv_ref), (k_sum, v_sum), squares)
        out_ref[rows, :128] = rope(
            k_sum[...] * scale, cos_ref[rows, :], sin_ref[rows, :]
        ).astype(jnp.bfloat16)
        out_ref[rows, 128:] = (v_sum[...] * scale).astype(jnp.bfloat16)
        return 0

    lax.fori_loop(0, 2, body, 0)


def q_kernel(gain_ref, dil_ref, width_ref, cos_ref, sin_ref, *refs):
    x_refs, (wq_ref, out_ref, list_ref, xbuf, q_sum, squares, sems) = refs[:10], refs[10:]
    fetch_features(x_refs, xbuf, sems)
    x0, z, core = seq_place()
    first = first_block_here()
    side = jnp.where(core == 0, ZS - 1, 1)

    def is_early(b):
        owner = b >> 2
        dz = ((owner >> 1) - z) & (ZS - 1)
        same = (owner >> 4) == x0
        near = jnp.where(((dz + 2) & (ZS - 1)) <= 4, 1, 0)
        across = jnp.where((dz == 0) | (dz == side), 1, 0)
        return jnp.where(same, near, across)

    def lists_of(j, _):
        i = first + j
        low = i - width_ref[j] + 1
        start = jnp.maximum(low, 0)

        def listed(t, counts):
            early, late = counts
            far = t < DILATION_COUNT
            b = jnp.where(
                far, dil_ref[i, jnp.minimum(t, DILATION_COUNT - 1)], start + t - DILATION_COUNT
            )
            list_ref[j, 1 + early] = b
            list_ref[j, LATE + 1 + late] = b
            valid = jnp.where(far & (b >= low), 0, 1)
            e = is_early(b)
            return early + valid * e, late + valid * (1 - e)

        early, late = lax.fori_loop(
            0, i - start + DILATION_COUNT, listed, (jnp.int32(0), jnp.int32(0))
        )
        list_ref[j, 0] = early
        list_ref[j, LATE] = late
        return 0

    lax.fori_loop(0, QB, lists_of, 0)

    def body(half, _):
        rows = pl.ds(pl.multiple_of(half * HALF, HALF), HALF)
        scale = project(xbuf, gain_ref, rows, (wq_ref,), (q_sum,), squares) * SCORE_FACTOR
        for g in range(4):
            cols = slice(g * 128, (g + 1) * 128)
            out_ref[rows, cols] = rope(
                q_sum[:, cols] * scale, cos_ref[rows, :], sin_ref[rows, :]
            ).astype(jnp.bfloat16)
        return 0

    lax.fori_loop(0, 2, body, 0)


def fetch(kv_in, sources, buf, sems):
    x0, z, core = seq_place()
    copies = []
    for ref, parts in zip(kv_in, sources):
        for s, part in enumerate(parts):
            dest = pl.multiple_of(seq_at(x0, z, core, part) * ROWS, ROWS)
            c = pltpu.make_async_copy(
                ref.at[pl.ds(s * ROWS, ROWS), :], buf.at[pl.ds(dest, ROWS), :], sems.at[len(copies)]
            )
            c.start()
            copies.append(c)
    return copies


def load(buf, blocks):
    keys, values = [], []
    for b in blocks:
        r = pl.ds(pl.multiple_of(b * BLOCK, BLOCK), BLOCK)
        keys.append(buf[r, :128])
        values.append(buf[r, 128:])
    ones = jnp.ones((GROUP * BLOCK, 128), jnp.bfloat16)
    values = jnp.concatenate(values, axis=0)
    return jnp.concatenate(keys, axis=0), jnp.concatenate([values, ones], axis=1)


def scored(q_ref, j, half, keys):
    rows = pl.ds(pl.multiple_of(j * BLOCK, BLOCK), BLOCK)
    q = jnp.concatenate(
        [
            q_ref[rows, pl.ds(pl.multiple_of((2 * half + c) * 128, 128), 128)]
            for c in range(2)
        ],
        axis=0,
    )
    return lax.dot_general(q, keys, (((1,), (1,)), ((), ())), preferred_element_type=jnp.float32)


def update(q_ref, j, at, buf, blocks, acc, top, limit=None):
    keys, values = load(buf, blocks)

    def one_half(half, _):
        s = scored(q_ref, j, half, keys)
        if limit is not None:
            col = lax.broadcasted_iota(jnp.int32, s.shape, 1)
            s = jnp.where(col < limit, s, NEGATIVE)
        old = top[at, half]
        new = jnp.maximum(old, jnp.max(s, axis=1, keepdims=True))
        fade = jnp.exp2(old - new)
        p = jnp.exp2(s - jnp.concatenate([new] * GROUP, axis=1)).astype(jnp.bfloat16)
        acc[at, half] = acc[at, half] * jnp.concatenate([fade] * 2, axis=1) + dot_f32(p, values)
        top[at, half] = new
        return 0

    lax.fori_loop(0, 2, one_half, 0, unroll=limit is None)


def early_kernel(base, list_ref, q_ref, *refs):
    n = len(EARLY_FROM)
    kv_in, (acc, top, buf, sems) = refs[:n], refs[n:]
    first_block = first_block_here()
    for c in fetch(kv_in, EARLY_FROM, buf, sems):
        c.wait()

    def one_block(at, _):
        j = base + at
        i = first_block + j
        total = list_ref[j, 0]
        rest = lax.rem(total, GROUP)
        keys, values = load(
            buf, [i] + [jnp.where(t < rest, list_ref[j, 1 + t], i) for t in range(GROUP - 1)]
        )
        shape = (2 * BLOCK, GROUP * BLOCK)
        col = lax.broadcasted_iota(jnp.int32, shape, 1)
        row = lax.broadcasted_iota(jnp.int32, shape, 0) & (BLOCK - 1)
        limit = jnp.where(col < BLOCK, row + 1, (1 + rest) * BLOCK)
        for half in range(2):
            s = jnp.where(col < limit, scored(q_ref, j, half, keys), NEGATIVE)
            m = jnp.max(s, axis=1, keepdims=True)
            p = jnp.exp2(s - m).astype(jnp.bfloat16)
            acc[at, half] = dot_f32(p, values)
            top[at, half] = jnp.broadcast_to(m, (2 * BLOCK, 128))

        def step(g, _):
            t = 1 + rest + g * GROUP
            update(q_ref, j, at, buf, [list_ref[j, t + e] for e in range(GROUP)], acc, top)
            return 0

        lax.fori_loop(0, lax.div(total, GROUP), step, 0)
        return 0

    lax.fori_loop(0, QB // 2, one_block, 0)


def late_kernel(base, list_ref, q_ref, acc_ref, top_ref, w_hbm, *refs):
    n = len(LATE_FROM)
    kv_in, out_refs = refs[:n], refs[n : n + 8]
    acc, top, attention, shares, w_ref, buf, sems = refs[n + 8 :]
    copies = fetch(kv_in, LATE_FROM, buf, sems)
    weights = pltpu.make_async_copy(w_hbm, w_ref, sems.at[len(copies)])
    weights.start()
    for source, target in ((acc_ref, acc), (top_ref, top)):
        c = pltpu.make_async_copy(source, target, sems.at[len(copies) + 1])
        c.start()
        copies.append(c)
    for c in copies:
        c.wait()

    def one_block(at, _):
        j = base + at
        total = list_ref[j, LATE]
        rest = lax.rem(total, GROUP)

        @pl.when(rest > 0)
        def _():
            first = list_ref[j, LATE + 1]
            blocks = [first] + [
                jnp.where(t < rest, list_ref[j, LATE + 1 + t], first) for t in range(1, GROUP)
            ]
            update(q_ref, j, at, buf, blocks, acc, top, rest * BLOCK)

        def step(g, _):
            t = LATE + 1 + rest + g * GROUP
            update(q_ref, j, at, buf, [list_ref[j, t + e] for e in range(GROUP)], acc, top)
            return 0

        lax.fori_loop(0, lax.div(total, GROUP), step, 0)
        rows = pl.ds(pl.multiple_of(at * BLOCK, BLOCK), BLOCK)
        for half in range(2):
            a = acc[at, half]
            o = (a[:, :128] / a[:, 128:]).astype(jnp.bfloat16)
            attention[rows, (2 * half) * 128 : (2 * half + 1) * 128] = o[:BLOCK]
            attention[rows, (2 * half + 1) * 128 : (2 * half + 2) * 128] = o[BLOCK:]
        return 0

    lax.fori_loop(0, QB // 2, one_block, 0)
    weights.wait()

    def share(h, _):
        w = w_ref[:, pl.ds(pl.multiple_of(h * 512, 512), 512)]
        shares[h] = dot_f32(attention[...], w).astype(bf16)
        return 0

    lax.fori_loop(0, 8, share, 0)
    copies = []
    for k, o in enumerate(out_refs):
        c = pltpu.make_async_copy(shares.at[head_at(FEATURE_FROM[k])], o, sems.at[k])
        c.start()
        copies.append(c)
    for c in copies:
        c.wait()


VMEM = pl.BlockSpec(memory_space=pltpu.VMEM)
SMEM = pl.BlockSpec(memory_space=pltpu.SMEM)
ANY = pl.BlockSpec(memory_space=pl.ANY)
bf16 = jnp.bfloat16


ACC = (QB // 2, 2, 2 * BLOCK, 256)
TOP = (QB // 2, 2, 2 * BLOCK, 128)


def attend_early(base, lists, q, early):
    return pl.pallas_call(
        functools.partial(early_kernel, base),
        out_shape=[jax.ShapeDtypeStruct(ACC, jnp.float32), jax.ShapeDtypeStruct(TOP, jnp.float32)],
        in_specs=[SMEM, VMEM] + [ANY] * len(early),
        out_specs=[VMEM] * 2,
        scratch_shapes=[pltpu.VMEM((32 * ROWS, 256), bf16), pltpu.SemaphoreType.DMA((32,))],
        cost_estimate=pl.CostEstimate(flops=5 * 10**9, transcendentals=10**6, bytes_accessed=4 * 10**6),
        name="attend_early",
    )(lists, q, *early)


def attend_late(base, lists, q, state, w_output, late):
    return pl.pallas_call(
        functools.partial(late_kernel, base),
        out_shape=[jax.ShapeDtypeStruct((HALF, 512), bf16)] * 8,
        in_specs=[SMEM, VMEM] + [ANY] * (3 + len(late)),
        out_specs=[ANY] * 8,
        scratch_shapes=[
            pltpu.VMEM(ACC, jnp.float32),
            pltpu.VMEM(TOP, jnp.float32),
            pltpu.VMEM((HALF, 512), bf16),
            pltpu.VMEM((8, HALF, 512), bf16),
            pltpu.VMEM((512, MODEL_WIDTH), bf16),
            pltpu.VMEM((32 * ROWS, 256), bf16),
            pltpu.SemaphoreType.DMA((32,)),
        ],
        cost_estimate=pl.CostEstimate(flops=5 * 10**9, transcendentals=10**6, bytes_accessed=10**7),
        name="attend_late",
    )(lists, q, *state, w_output, *late)


def shards(tokens, norm_gain, w_query, w_key, w_value, w_output, widths, dilation):
    half_size = HEAD_WIDTH // 2
    positions = first_block_here() * BLOCK + jnp.arange(ROWS, dtype=jnp.int32)
    frequency = ROPE_BASE ** (-jnp.arange(half_size, dtype=jnp.float32) * 2.0 / HEAD_WIDTH)
    angles = positions.astype(jnp.float32)[:, None] * frequency[None, :]
    cosine, sine = jnp.cos(angles), jnp.sin(angles)
    cosine = jnp.concatenate([cosine, cosine], axis=1)
    sine = jnp.concatenate([-sine, sine], axis=1)
    gain = norm_gain.reshape(8, 512)

    full, quarter = gather_features(tokens)
    pieces = full + quarter
    kv = pl.pallas_call(
        kv_kernel,
        out_shape=jax.ShapeDtypeStruct((ROWS, 256), bf16),
        in_specs=[VMEM] * 3 + [ANY] * 10 + [VMEM] * 2,
        out_specs=VMEM,
        scratch_shapes=[
            pltpu.VMEM((8, ROWS, 512), bf16),
            pltpu.VMEM((HALF, 128), jnp.float32),
            pltpu.VMEM((HALF, 128), jnp.float32),
            pltpu.VMEM((HALF, 128), jnp.float32),
            pltpu.SemaphoreType.DMA((10,)),
        ],
        cost_estimate=pl.CostEstimate(flops=10**9, transcendentals=0, bytes_accessed=6 * 10**6),
        name="keys_values",
    )(gain, cosine, sine, *pieces, w_key, w_value)
    early, late = gather_blocks(kv)
    query_call = pl.pallas_call(
        q_kernel,
        out_shape=[
            jax.ShapeDtypeStruct((ROWS, 512), bf16),
            jax.ShapeDtypeStruct((QB, 2 * LATE), jnp.int32),
        ],
        in_specs=[VMEM] + [SMEM] * 2 + [VMEM] * 2 + [ANY] * 10 + [VMEM],
        out_specs=[VMEM, SMEM],
        scratch_shapes=[
            pltpu.VMEM((8, ROWS, 512), bf16),
            pltpu.VMEM((HALF, 512), jnp.float32),
            pltpu.VMEM((HALF, 128), jnp.float32),
            pltpu.SemaphoreType.DMA((10,)),
        ],
        cost_estimate=pl.CostEstimate(flops=4 * 10**9, transcendentals=0, bytes_accessed=10**7),
        name="queries",
    )
    q, lists = query_call(gain, dilation, widths, cosine, sine, *pieces, w_query)
    states = [attend_early(k * QB // 2, lists, q, early) for k in range(2)]
    outs = []
    for k in range(2):
        shares = attend_late(k * QB // 2, lists, q, states[k], w_output, late)
        outs.append(scatter_sums(shares, tokens[k * HALF : (k + 1) * HALF]))
    return cat(*outs)


def solution(mesh):
    split = Mesh(mesh.devices.reshape(2, ZS, 2, YS, XS), SEQ + HEAD)
    placed = (
        P(SEQ, HEAD),
        P(),
        P(None, HEAD),
        P(None, HEAD),
        P(None, HEAD),
        P(HEAD, None),
        P(SEQ),
        P(),
    )
    return jax.shard_map(
        shards, mesh=split, in_specs=placed, out_specs=P(SEQ, HEAD), check_vma=False
    )
```

```python
import functools
import math

import jax
import jax.numpy as jnp
from jax import lax
from jax.experimental import pallas as pl
from jax.experimental.pallas import tpu as pltpu
from jax.sharding import Mesh
from jax.sharding import PartitionSpec as P

MODEL_WIDTH = 4096
HEAD_WIDTH = 128
BLOCK = 128
DILATION_COUNT = 8
ROWS = 512
HALF = 256
QB = 4
SEQ = ("seq_0", "seq_1", "seq_2")
HEAD = ("head_0", "head_1")
YS, XS, ZS = 4, 2, 8
EPSILON = 1e-05
NEGATIVE = -1e30
ROPE_BASE = 10000.0
SCORE_FACTOR = math.log2(math.e) / math.sqrt(HEAD_WIDTH)
GROUP = 4


def moved(x, axis, size, step):
    return lax.ppermute(x, axis, [(k, (k + step) % size) for k in range(size)])


def y_up(x):
    return moved(x, "head_0", YS, 1)


def y_down(x):
    return moved(x, "head_0", YS, -1)


def x_flip(x):
    return moved(x, "head_1", XS, 1)


def pair_flip(x):
    return moved(x, "seq_0", 2, 1)


def core_flip(x):
    return moved(x, "seq_2", 2, 1)


def gather_features(a):
    n = a.shape[0] // 2
    b = x_flip(a)
    u = y_up(a)
    d = y_down(a)
    ct = y_up(u[:n])
    cb = y_down(d[n:])
    bu = y_up(b)
    bd = y_down(b)
    et = x_flip(ct)
    eb = x_flip(cb)
    return (a, b, u, d, bu, bd), (ct, cb, et, eb)


FEATURE_FROM = ((0, 0), (0, 1), (-1, 0), (1, 0), (-1, 1), (1, 1), (2, 0), (2, 1))


def ring(x):
    pairs = []
    for z in range(ZS):
        pairs.append((2 * z, 2 * ((z + 1) % ZS)))
        pairs.append((2 * z + 1, 2 * ((z - 1) % ZS) + 1))
    return lax.ppermute(x, ("seq_1", "seq_2"), pairs)


def cat(*v):
    return jnp.concatenate(v, axis=0)


def gather_blocks(k):
    n = k.shape[0]
    k2 = cat(k, core_flip(k))
    b = pair_flip(k)
    r1 = ring(k2)
    b2 = cat(b, core_flip(b))
    r2 = ring(r1)
    rb1 = ring(b2)
    r3 = ring(r2)
    s1 = core_flip(cat(r1, r2))
    rb2 = ring(rb1)
    r4 = ring(r3[:n])
    f3 = pair_flip(r3)
    s2 = core_flip(cat(rb1, r3, r4))
    f4 = pair_flip(r4)
    s3 = core_flip(cat(rb2, f3, f4))
    return k2, b2, r1, r2, rb1, r3, r4, rb2, f3, f4, s1, s2, s3


PARTS_OF = {
    "k2": ((0, 0, 0), (0, 0, 1)),
    "b2": ((1, 0, 0), (1, 0, 1)),
    "r1": ((0, 1, 0), (0, 1, 1)),
    "r2": ((0, 2, 0), (0, 2, 1)),
    "rb1": ((1, 1, 0), (1, 1, 1)),
    "r3": ((0, 3, 0), (0, 3, 1)),
    "r4": ((0, 4, 0),),
    "rb2": ((1, 2, 0), (1, 2, 1)),
    "f3": ((1, 3, 0), (1, 3, 1)),
    "f4": ((1, 4, 0),),
}
BLOCK_FROM = tuple(
    tuple((dx, steps, c, 0) for dx, steps, c in PARTS_OF[name])
    for name in ("k2", "b2", "r1", "r2", "rb1", "r3", "r4", "rb2", "f3", "f4")
) + tuple(
    tuple((dx, steps, 1 - c, 1) for name in names for dx, steps, c in PARTS_OF[name])
    for names in (("r1", "r2"), ("rb1", "r3", "r4"), ("rb2", "f3", "f4"))
)


def seq_at(x0, z, core, part):
    dx, steps, other, far_ring = part
    turn = jnp.where((core + far_ring) % 2 == 0, ZS - steps, steps)
    return ((x0 + dx) % 2 * ZS + (z + turn) % ZS) * 2 + (core + other) % 2


def add_up(first, *rest):
    total = first.astype(jnp.float32)
    for r in rest:
        total = total + r.astype(jnp.float32)
    return total


def scatter_sums(part, residual):
    p = dict(zip(FEATURE_FROM, part))
    n = residual.shape[0] // 2
    bf = jnp.bfloat16
    far = x_flip(p[(2, 1)])
    from_low = y_up(p[(1, 1)])
    from_high = y_down(p[(-1, 1)])
    c = add_up(p[(2, 0)], far).astype(bf)
    c_low = y_up(c[:n])
    c_high = y_down(c[n:])
    rx = x_flip(add_up(p[(0, 1)], from_low, from_high).astype(bf))
    up = p[(1, 0)]
    down = p[(-1, 0)]
    up = jnp.concatenate([add_up(up[:n], c_low).astype(bf), up[n:]], axis=0)
    down = jnp.concatenate([down[:n], add_up(down[n:], c_high).astype(bf)], axis=0)
    ru = y_up(up)
    rd = y_down(down)
    return add_up(residual, p[(0, 0)], rx, ru, rd).astype(bf)


def dot_f32(a, b):
    return jnp.dot(a, b, preferred_element_type=jnp.float32)


def seq_place():
    return tuple(lax.axis_index(a) for a in SEQ)


def first_block_here():
    x0, z, core = seq_place()
    return ((x0 * ZS + z) * 2 + core) * QB


def head_at(part):
    y, xh = lax.axis_index("head_0"), lax.axis_index("head_1")
    dy, dx = part
    return (y + (dy + YS) % YS) % YS * XS + (xh + dx) % XS


def joined(quarter, whole):
    for k in range(2):
        for half in range(2):
            whole[k, half * HALF : (half + 1) * HALF, :] = quarter[2 * k + half][...]


def project(gain_ref, full, whole, rows, weights):
    squares = jnp.zeros((HALF, 128), jnp.float32)
    sums = [jnp.zeros((HALF, w.shape[1]), jnp.float32) for w in weights]
    for k, part in enumerate(FEATURE_FROM):
        piece = full[k][rows, :] if k < 6 else whole[k - 6, rows, :]
        h = head_at(part)
        x = piece.astype(jnp.float32)
        x2 = x * x
        for c in range(4):
            squares = squares + x2[:, c * 128 : (c + 1) * 128]
        scaled = (x * gain_ref[pl.ds(h, 1), :]).astype(jnp.bfloat16)
        span = pl.ds(pl.multiple_of(h * 512, 512), 512)
        for j, w in enumerate(weights):
            sums[j] = sums[j] + dot_f32(scaled, w[span, :])
    total = jnp.sum(squares, axis=1, keepdims=True)
    return sums, lax.rsqrt(total * (1.0 / MODEL_WIDTH) + EPSILON)


def rope(u, cos, sin):
    return u * cos + pltpu.roll(u, 64, 1) * sin


def kv_kernel(gain_ref, cos_ref, sin_ref, *refs):
    full, quarter, (wk_ref, wv_ref, out_ref, whole) = refs[:6], refs[6:10], refs[10:]
    joined(quarter, whole)

    def body(half, _):
        rows = pl.ds(pl.multiple_of(half * HALF, HALF), HALF)
        (k, v), scale = project(gain_ref, full, whole, rows, (wk_ref, wv_ref))
        out_ref[rows, :128] = rope(k * scale, cos_ref[rows, :], sin_ref[rows, :]).astype(jnp.bfloat16)
        out_ref[rows, 128:] = (v * scale).astype(jnp.bfloat16)
        return 0

    lax.fori_loop(0, 2, body, 0)


def q_kernel(gain_ref, dil_ref, width_ref, cos_ref, sin_ref, *refs):
    full, quarter, (wq_ref, out_ref, list_ref, whole) = refs[:6], refs[6:10], refs[10:]
    joined(quarter, whole)
    first = first_block_here()
    for j in range(QB):
        i = first + j
        low = i - width_ref[j] + 1
        start = jnp.maximum(low, 0)
        count = jnp.int32(0)
        for e in range(DILATION_COUNT):
            b = dil_ref[i, e]
            list_ref[j, 1 + count] = b
            count = count + jnp.where(b < low, 1, 0)

        def near(t, _):
            list_ref[j, 1 + count + t] = start + t
            return 0

        lax.fori_loop(0, i - start, near, 0)
        list_ref[j, 0] = count + i - start

    def body(half, _):
        rows = pl.ds(pl.multiple_of(half * HALF, HALF), HALF)
        (q,), scale = project(gain_ref, full, whole, rows, (wq_ref,))
        scale = scale * SCORE_FACTOR
        for g in range(4):
            cols = slice(g * 128, (g + 1) * 128)
            out_ref[rows, cols] = rope(
                q[:, cols] * scale, cos_ref[rows, :], sin_ref[rows, :]
            ).astype(jnp.bfloat16)
        return 0

    lax.fori_loop(0, 2, body, 0)


def out_kernel(which, at_ref, w_hbm, *refs):
    out_refs, (w_ref, sems) = refs[: len(which)], refs[len(which) :]
    copies = []
    for n, k in enumerate(which):
        cols = pl.ds(pl.multiple_of(head_at(FEATURE_FROM[k]) * 512, 512), 512)
        c = pltpu.make_async_copy(w_hbm.at[:, cols], w_ref.at[n], sems.at[n])
        c.start()
        copies.append(c)
    for n, o in enumerate(out_refs):
        copies[n].wait()
        o[...] = dot_f32(at_ref[...], w_ref[n]).astype(jnp.bfloat16)


def attention_kernel(list_ref, q_ref, *refs):
    kv_in, (out_ref, buf, acc, top, sems) = refs[: len(BLOCK_FROM)], refs[len(BLOCK_FROM) :]
    x0, z, core = seq_place()
    first_block = first_block_here()
    copies = []
    for ref, parts in zip(kv_in, BLOCK_FROM):
        for s, part in enumerate(parts):
            dest = pl.multiple_of(seq_at(x0, z, core, part) * ROWS, ROWS)
            c = pltpu.make_async_copy(
                ref.at[pl.ds(s * ROWS, ROWS), :], buf.at[pl.ds(dest, ROWS), :], sems.at[len(copies)]
            )
            c.start()
            copies.append(c)
    for c in copies:
        c.wait()
    ones = jnp.ones((GROUP * BLOCK, 128), jnp.bfloat16)

    def load(blocks):
        keys, values = [], []
        for b in blocks:
            r = pl.ds(pl.multiple_of(b * BLOCK, BLOCK), BLOCK)
            keys.append(buf[r, :128])
            values.append(buf[r, 128:])
        values = jnp.concatenate(values, axis=0)
        return jnp.concatenate(keys, axis=0), jnp.concatenate([values, ones], axis=1)

    def one_block(j, _):
        i = first_block + j
        total = list_ref[j, 0]
        rest = lax.rem(total, GROUP)
        rows = pl.ds(pl.multiple_of(j * BLOCK, BLOCK), BLOCK)

        def queries(half):
            return jnp.concatenate(
                [q_ref[rows, c * 128 : (c + 1) * 128] for c in (2 * half, 2 * half + 1)], axis=0
            )

        keys, values = load(
            [i] + [jnp.where(t < rest, list_ref[j, 1 + t], i) for t in range(GROUP - 1)]
        )
        shape = (2 * BLOCK, GROUP * BLOCK)
        col = lax.broadcasted_iota(jnp.int32, shape, 1)
        row = lax.broadcasted_iota(jnp.int32, shape, 0) & (BLOCK - 1)
        limit = jnp.where(col < BLOCK, row + 1, (1 + rest) * BLOCK)
        for half in range(2):
            s = lax.dot_general(
                queries(half), keys, (((1,), (1,)), ((), ())), preferred_element_type=jnp.float32
            )
            s = jnp.where(col < limit, s, NEGATIVE)
            m = jnp.max(s, axis=1, keepdims=True)
            p = jnp.exp2(s - m).astype(jnp.bfloat16)
            acc[half] = dot_f32(p, values)
            top[half] = jnp.broadcast_to(m, (2 * BLOCK, 128))

        def step(g, _):
            t = 1 + rest + g * GROUP
            keys, values = load([list_ref[j, t + e] for e in range(GROUP)])
            for half in range(2):
                s = lax.dot_general(
                    queries(half), keys, (((1,), (1,)), ((), ())), preferred_element_type=jnp.float32
                )
                old = top[half]
                new = jnp.maximum(old, jnp.max(s, axis=1, keepdims=True))
                fade = jnp.exp2(old - new)
                p = jnp.exp2(s - jnp.concatenate([new] * GROUP, axis=1)).astype(jnp.bfloat16)
                acc[half] = acc[half] * jnp.concatenate([fade] * 2, axis=1) + dot_f32(p, values)
                top[half] = new
            return 0

        lax.fori_loop(0, lax.div(total, GROUP), step, 0)
        for half in range(2):
            a = acc[half]
            o = (a[:, :128] / a[:, 128:]).astype(jnp.bfloat16)
            out_ref[rows, (2 * half) * 128 : (2 * half + 1) * 128] = o[:BLOCK]
            out_ref[rows, (2 * half + 1) * 128 : (2 * half + 2) * 128] = o[BLOCK:]
        return 0

    lax.fori_loop(0, QB, one_block, 0)


VMEM = pl.BlockSpec(memory_space=pltpu.VMEM)
SMEM = pl.BlockSpec(memory_space=pltpu.SMEM)
ANY = pl.BlockSpec(memory_space=pl.ANY)
bf16 = jnp.bfloat16


def local_attention(lists, q, gathered):
    return pl.pallas_call(
        attention_kernel,
        out_shape=jax.ShapeDtypeStruct((ROWS, 512), bf16),
        in_specs=[SMEM, VMEM] + [ANY] * len(gathered),
        out_specs=VMEM,
        scratch_shapes=[
            pltpu.VMEM((32 * ROWS, 256), bf16),
            pltpu.VMEM((2, 2 * BLOCK, 256), jnp.float32),
            pltpu.VMEM((2, 2 * BLOCK, 128), jnp.float32),
            pltpu.SemaphoreType.DMA((32,)),
        ],
        cost_estimate=pl.CostEstimate(flops=2 * 10**10, transcendentals=10**7, bytes_accessed=10**7),
        compiler_params=pltpu.CompilerParams(vmem_limit_bytes=24 << 20),
        name="attend",
    )(lists, q, *gathered)


def shards(tokens, norm_gain, w_query, w_key, w_value, w_output, widths, dilation):
    half_size = HEAD_WIDTH // 2
    positions = first_block_here() * BLOCK + jnp.arange(ROWS, dtype=jnp.int32)
    frequency = ROPE_BASE ** (-jnp.arange(half_size, dtype=jnp.float32) * 2.0 / HEAD_WIDTH)
    angles = positions.astype(jnp.float32)[:, None] * frequency[None, :]
    cosine, sine = jnp.cos(angles), jnp.sin(angles)
    cosine = jnp.concatenate([cosine, cosine], axis=1)
    sine = jnp.concatenate([-sine, sine], axis=1)
    gain = norm_gain.reshape(8, 512)

    full, quarter = gather_features(tokens)
    pieces = full + quarter
    kv = pl.pallas_call(
        kv_kernel,
        out_shape=jax.ShapeDtypeStruct((ROWS, 256), bf16),
        in_specs=[VMEM] * 15,
        out_specs=VMEM,
        scratch_shapes=[pltpu.VMEM((2, ROWS, 512), bf16)],
        cost_estimate=pl.CostEstimate(flops=10**9, transcendentals=0, bytes_accessed=6 * 10**6),
        compiler_params=pltpu.CompilerParams(vmem_limit_bytes=20 << 20),
        name="keys_values",
    )(gain, cosine, sine, *pieces, w_key, w_value)
    gathered = gather_blocks(kv)
    query_call = pl.pallas_call(
        q_kernel,
        out_shape=[
            jax.ShapeDtypeStruct((ROWS, 512), bf16),
            jax.ShapeDtypeStruct((QB, 64), jnp.int32),
        ],
        in_specs=[VMEM] + [SMEM] * 2 + [VMEM] * 13,
        out_specs=[VMEM, SMEM],
        scratch_shapes=[pltpu.VMEM((2, ROWS, 512), bf16)],
        cost_estimate=pl.CostEstimate(flops=4 * 10**9, transcendentals=0, bytes_accessed=10**7),
        compiler_params=pltpu.CompilerParams(vmem_limit_bytes=24 << 20),
        name="queries",
    )
    q, lists = query_call(gain, dilation, widths, cosine, sine, *pieces, w_query)
    attention = local_attention(lists, q, gathered)

    def shares(which):
        return pl.pallas_call(
            functools.partial(out_kernel, which),
            out_shape=[jax.ShapeDtypeStruct((ROWS, 512), bf16)] * len(which),
            in_specs=[VMEM, ANY],
            out_specs=[VMEM] * len(which),
            scratch_shapes=[
                pltpu.VMEM((len(which), 512, 512), bf16),
                pltpu.SemaphoreType.DMA((len(which),)),
            ],
            cost_estimate=pl.CostEstimate(
                flops=len(which) * 2**28, transcendentals=0, bytes_accessed=len(which) * 2**20
            ),
            compiler_params=pltpu.CompilerParams(vmem_limit_bytes=16 << 20),
            name="project_out",
        )(attention, w_output)

    part = {}
    for which in ((7,), (4, 5), (6, 1, 2, 3, 0)):
        part.update(zip(which, shares(which)))
    return scatter_sums([part[k] for k in range(8)], tokens)


def solution(mesh):
    split = Mesh(mesh.devices.reshape(2, ZS, 2, YS, XS), SEQ + HEAD)
    placed = (
        P(SEQ, HEAD),
        P(),
        P(None, HEAD),
        P(None, HEAD),
        P(None, HEAD),
        P(HEAD, None),
        P(SEQ),
        P(),
    )
    return jax.shard_map(
        shards, mesh=split, in_specs=placed, out_specs=P(SEQ, HEAD), check_vma=False
    )
```
